256 devices in a mesh: prow: 32 (over y, x, core), pcol: 8 (over z).
Axes of the slice: x: 4, y: 4, z: 8, core: 2. Of those that a mesh axis runs over, the one named last changes fastest.
Arguments:
- designs: float32 [8192, 64], P('prow'), may hold values from -4 to 4
- length_weights: float32 [64], replicated, may hold values from 0.002 to 0.03
- trailing: float32 [16384, 16384], P('prow', 'pcol'), as said below
Outputs:
- updated_trailing: float32 [16384, 16384], P('prow', 'pcol')
- panel_rows: float32 [16384, 512], P('prow', 'pcol')
- panel_factor: float32 [512, 512], P(None, 'pcol')
The draws below stay inside these ranges and needn't reach their ends.
Inputs may be any that keep to these rules, and one draw needn't show every extreme that they name: `trailing`: symmetric.
All inputs are finite; a program needn't handle non-finite values.
Results may differ from the reference program's by a relative error of at most 0.0003.
Values sent between devices are 32-bit elements; how exact they have to be, the bound alone decides.
No kernel may reach another device: no remote copies, remote signals or barrier semaphores. Data moves between devices by JAX's collectives and lax.ppermute only.
A program may use at most 128 MiB of HBM per device.

```python
import math
import jax
import jax.numpy as jnp
from jax import lax

DIM = 64
PANEL = 512
DESIGNS = 8192
TRAIL = 16384


def draw_trailing(key, part):
    noise_key = jax.random.fold_in(key, 11)
    diag_key = jax.random.fold_in(key, 12)
    noise = jnp.clip(jax.random.normal(noise_key, (TRAIL, TRAIL), jnp.float32), -6.0, 6.0)
    symmetric = (noise + noise.T) * 0.15
    diagonal = jax.random.uniform(diag_key, (TRAIL,), jnp.float32, 1.0, 4.0)
    return symmetric + jnp.diag(diagonal)


def shard_levels(own_key, extent, cuts, low, high):
    factor_of, own = 1.0, jax.random.fold_in(own_key, 6)
    for axis_at, shards_of in cuts:
        steps = jnp.exp(jax.random.uniform(jax.random.fold_in(own, axis_at), (shards_of,), jnp.float32, low / len(cuts), high / len(cuts)))
        factor_of = factor_of * jnp.repeat(steps, extent[axis_at] // shards_of).reshape([-1 if axis == axis_at else 1 for axis in range(len(extent))])
    return factor_of


def normal_values(key, dims, spread, limit, shards=(), kind=jnp.bfloat16):
    result = spread * jax.random.normal(key, dims, jnp.float32)
    if shards:
        result = result * shard_levels(key, dims, shards, -0.22, 0.18)
    return jnp.clip(result, -limit, limit).astype(kind)


def setup_inputs(seed: int = 0) -> dict:
    key_of = jax.random.split(jax.random.key(seed), 4)
    return {
        "designs": normal_values(key_of[0], (DESIGNS, DIM), 1.0, 4.0, ((0, 32),), jnp.float32),
        "length_weights": jnp.clip(jnp.exp(jax.random.uniform(key_of[1], (DIM,), jnp.float32, math.log(0.002), math.log(0.03))), 0.002, 0.03),
        "trailing": draw_trailing(jax.random.fold_in(key_of[3], 71), 0),
    }


signal_variance = 4.0
nugget_level = 0.1

def scaled_pair(row_points, panel_points, length_weights):
    root_weights = jnp.sqrt(length_weights)
    return (row_points * root_weights, panel_points * root_weights)

def kernel_values(scaled_rows, scaled_panel):
    inner_terms = jnp.dot(scaled_rows, scaled_panel.T, precision=lax.Precision.HIGHEST)
    squares_rows = lax.optimization_barrier(jnp.sum(scaled_rows * scaled_rows, axis=1))[:, None]
    squares_panel = lax.optimization_barrier(jnp.sum(scaled_panel * scaled_panel, axis=1))[None, :]
    return signal_variance * jnp.exp(-(squares_rows + squares_panel - 2.0 * inner_terms))

def cross_block(row_points, panel_points, length_weights):
    scaled_rows, scaled_panel = scaled_pair(row_points, panel_points, length_weights)
    kernel = kernel_values(scaled_rows, scaled_panel)
    panel_gap = scaled_rows[:, -2][:, None] - scaled_panel[:, -2][None, :]
    trail_gap = scaled_rows[:, -1][:, None] - scaled_panel[:, -1][None, :]
    derivative_rows = -2.0 * kernel * trail_gap * panel_gap
    value_rows = math.sqrt(2.0) * kernel * panel_gap
    stacked = jnp.stack([derivative_rows, value_rows], axis=1)
    return stacked.reshape(2 * row_points.shape[0], panel_points.shape[0])

def diagonal_block(row_points, panel_points, length_weights, offset):
    scaled_rows, scaled_panel = scaled_pair(row_points, panel_points, length_weights)
    kernel = kernel_values(scaled_rows, scaled_panel)
    panel_gap = scaled_rows[:, -2][:, None] - scaled_panel[:, -2][None, :]
    row_iota = lax.broadcasted_iota(jnp.int32, kernel.shape, 0)
    col_iota = lax.broadcasted_iota(jnp.int32, kernel.shape, 1) + offset
    return kernel * (1.0 - 2.0 * panel_gap * panel_gap) + jnp.where(row_iota == col_iota, nugget_level, 0.0)

def reference(designs, length_weights, trailing):
    panel_points = designs[DESIGNS - PANEL:]
    block = diagonal_block(panel_points, panel_points, length_weights, 0)
    panel_factor = jnp.linalg.cholesky(block)
    cross = cross_block(designs, panel_points, length_weights)
    panel_rows = jax.scipy.linalg.solve_triangular(panel_factor, cross.T, lower=True).T
    updated = trailing - jnp.dot(panel_rows, panel_rows.T, precision=lax.Precision.HIGHEST)
    return (updated, panel_rows, panel_factor)
```

```python
import math

import jax
import jax.numpy as jnp
from jax import lax
from jax.experimental import pallas as pl
from jax.experimental.pallas import tpu as pltpu
from jax.sharding import PartitionSpec as P

PANEL = 512
DIM = 64
BLOCK = 128
GROUP = 8

signal_variance = 4.0
nugget_level = 0.1

F32 = jnp.float32
BF16 = jnp.bfloat16
HIGHEST = lax.Precision.HIGHEST
NT = (((1,), (1,)), ((), ()))
NN = (((1,), (0,)), ((), ()))


def dot_nt(a, b):
    return lax.dot_general(a, b, NT, precision=HIGHEST, preferred_element_type=F32)


def dot_nn(a, b):
    return lax.dot_general(a, b, NN, precision=HIGHEST, preferred_element_type=F32)


def split(x):
    hi = x.astype(BF16)
    return hi, (x - hi.astype(F32)).astype(BF16)


def dot_split(a, b):
    one = lambda p, q: lax.dot_general(p, q, NT, preferred_element_type=F32)
    return one(a[0], b[0]) + (one(a[0], b[1]) + one(a[1], b[0]))


def lane_spread(x, lane):
    return jnp.broadcast_to(x[:, lane : lane + 1], (8, 128))


def row_spread(x, row):
    return jnp.broadcast_to(x[row : row + 1, :], (8, 128))


def factor_block(rows):
    lane = lax.broadcasted_iota(jnp.int32, (8, 128), 1)
    sub = lax.broadcasted_iota(jnp.int32, (8, 128), 0)
    rows = list(rows)
    for g in range(len(rows)):
        base = GROUP * g
        slab = rows[g]
        cols = [lane_spread(slab, base + j) for j in range(GROUP)]
        s = [[row_spread(cols[j], k) if k <= j else None for j in range(GROUP)] for k in range(GROUP)]
        r = [None] * GROUP
        u = [[None] * GROUP for _ in range(GROUP)]
        for k in range(GROUP):
            r[k] = lax.rsqrt(s[k][k])
            for j in range(k + 1, GROUP):
                u[k][j] = s[k][j] * r[k]
            for i in range(k + 1, GROUP):
                for j in range(i, GROUP):
                    s[i][j] = s[i][j] - u[k][i] * u[k][j]
        pivots = []
        final = slab
        for k in range(GROUP):
            row = row_spread(slab, k)
            for m in range(k):
                row = row - u[m][k] * pivots[m]
            row = row * r[k]
            diag = lane == base + k
            final = jnp.where(sub == k, jnp.where(diag, r[k], row), final)
            pivots.append(jnp.where(diag, s[k][k] * r[k] + r[k], row))
        rows[g] = final
        for i in range(g + 1, len(rows)):
            x = rows[i]
            c = [lane_spread(x, base + j) for j in range(GROUP)]
            for k in range(GROUP):
                low = c[k] * r[k]
                for j in range(k + 1, GROUP):
                    c[j] = c[j] - low * u[k][j]
                x = x - low * pivots[k]
            rows[i] = x
    return rows


def row_forms(points):
    shape = (8, DIM)
    sub = lax.broadcasted_iota(jnp.int32, shape, 0)
    lane = lax.broadcasted_iota(jnp.int32, shape, 1)
    pick = jnp.where(lane == DIM - 2 + sub, 1.0, 0.0).astype(F32)
    picked = dot_nt(pick, points)
    squares = dot_nt(jnp.ones(shape, F32), points * points)
    return squares[0:1], picked[0:1], picked[1:2]


def kernel_values(rows, points, squares_points):
    squares_rows = jnp.sum(rows * rows, axis=1, keepdims=True)
    gaps = squares_rows + squares_points - 2.0 * dot_nt(rows, points)
    return signal_variance * jnp.exp(-gaps)


def factor_kernel(panel_ref, weights_ref, factor_ref, inverse_ref, work_ref, block_ref):
    points = panel_ref[...] * jnp.sqrt(weights_ref[...])
    squares, along_u, _ = row_forms(points)
    kernel = kernel_values(points, points, squares)
    gap = points[:, DIM - 2 : DIM - 1] - along_u
    row_iota = lax.broadcasted_iota(jnp.int32, (PANEL, PANEL), 0)
    col_iota = lax.broadcasted_iota(jnp.int32, (PANEL, PANEL), 1)
    work_ref[...] = kernel * (1.0 - 2.0 * gap * gap) + jnp.where(row_iota == col_iota, nugget_level, 0.0)
    factor_ref[...] = jnp.zeros_like(factor_ref)
    inverse_ref[...] = jnp.zeros_like(inverse_ref)

    @pl.loop(0, PANEL // BLOCK)
    def _(step):
        at = pl.multiple_of(step * BLOCK, BLOCK)
        rows = [work_ref[pl.ds(at + 8 * i, 8), pl.ds(at, BLOCK)] for i in range(BLOCK // 8)]
        rows = factor_block(rows)
        for i in range(BLOCK // 8):
            block_ref[8 * i : 8 * i + 8, :] = rows[i]
        both = block_ref[...]
        r = lax.broadcasted_iota(jnp.int32, (BLOCK, BLOCK), 0)
        c = lax.broadcasted_iota(jnp.int32, (BLOCK, BLOCK), 1)
        upper = jnp.where(c > r, both, jnp.where(c == r, 1.0 / both, 0.0))
        factor_ref[pl.ds(at, BLOCK), pl.ds(at, BLOCK)] = upper.T
        inverse = jnp.where(c <= r, both, 0.0)
        inverse_ref[pl.ds(at, BLOCK), pl.ds(at, BLOCK)] = inverse
        for s in range(PANEL // BLOCK - 1):

            @pl.when(step == s)
            def _():
                end = BLOCK * (s + 1)
                below = dot_nt(work_ref[end:, end - BLOCK : end], inverse)
                factor_ref[end:, end - BLOCK : end] = below
                work_ref[end:, end:] = work_ref[end:, end:] - dot_nt(below, below)

    for n in (BLOCK, 2 * BLOCK):
        for t in range(0, PANEL, 2 * n):
            left = dot_nn(factor_ref[t + n : t + 2 * n, t : t + n], inverse_ref[t : t + n, t : t + n])
            inverse_ref[t + n : t + 2 * n, t : t + n] = -dot_nn(
                inverse_ref[t + n : t + 2 * n, t + n : t + 2 * n], left
            )


def factor_call(panel_points, weights):
    square = jax.ShapeDtypeStruct((PANEL, PANEL), F32)
    return pl.pallas_call(
        factor_kernel,
        out_shape=[square, square],
        scratch_shapes=[pltpu.VMEM((PANEL, PANEL), F32), pltpu.VMEM((BLOCK, BLOCK), F32)],
        compiler_params=pltpu.CompilerParams(vmem_limit_bytes=32 << 20),
        name="panel_factor",
    )(panel_points, weights)


def solved_rows(designs, weights, points, squares, along_u, along_v, inverse, cross_ref):
    rows = designs * jnp.sqrt(weights)
    kernel = kernel_values(rows, points, squares)
    gap_u = rows[:, DIM - 2 : DIM - 1] - along_u
    gap_v = rows[:, DIM - 1 : DIM] - along_v
    n = designs.shape[0]
    derivative = -2.0 * kernel * gap_v * gap_u
    value = math.sqrt(2.0) * kernel * gap_u
    for q in range(PANEL // 128):
        cross_ref[q, pl.ds(0, n, stride=2), :] = derivative[:, 128 * q : 128 * q + 128]
        cross_ref[q, pl.ds(1, n, stride=2), :] = value[:, 128 * q : 128 * q + 128]
    cross = jnp.concatenate([cross_ref[q] for q in range(PANEL // 128)], 1)
    return dot_split(split(cross), inverse)


def update_kernel(
    own_ref, far_ref, panel_ref, weights_ref, inverse_ref, trailing_ref,
    updated_ref, rows_ref, points_ref, forms_ref, inv_hi_ref, inv_lo_ref, row_hi_ref, row_lo_ref, cross_ref,
):
    weights = weights_ref[...]

    def solve(designs):
        forms = forms_ref[...]
        return solved_rows(
            designs, weights, points_ref[...], forms[0:1], forms[1:2], forms[2:3],
            (inv_hi_ref[...], inv_lo_ref[...]), cross_ref,
        )

    @pl.when(pl.program_id(0) == 0)
    def _():
        points = panel_ref[...] * jnp.sqrt(weights)
        points_ref[...] = points
        squares, along_u, along_v = row_forms(points)
        forms_ref[0:1, :] = squares
        forms_ref[1:2, :] = along_u
        forms_ref[2:3, :] = along_v
        hi, lo = split(inverse_ref[...])
        inv_hi_ref[...] = hi
        inv_lo_ref[...] = lo
        own = solve(own_ref[...])
        rows_ref[...] = own
        hi, lo = split(own)
        row_hi_ref[...] = hi
        row_lo_ref[...] = lo

    far = split(solve(far_ref[...]))
    updated_ref[...] = trailing_ref[...] - dot_split((row_hi_ref[...], row_lo_ref[...]), far)


def update_call(designs, far_designs, panel_points, weights, inverse, trailing):
    n = designs.shape[0]
    height, width = trailing.shape
    steps = far_designs.shape[0] // n
    whole = lambda *shape: pl.BlockSpec(shape, lambda j: (0,) * len(shape))
    tile = pl.BlockSpec((height, width // steps), lambda j: (0, j))
    return pl.pallas_call(
        update_kernel,
        grid=(steps,),
        in_specs=[
            whole(n, DIM), pl.BlockSpec((n, DIM), lambda j: (j, 0)), whole(PANEL, DIM), whole(1, DIM),
            whole(PANEL, PANEL), tile,
        ],
        out_specs=[tile, whole(height, PANEL)],
        out_shape=[jax.ShapeDtypeStruct((height, width), F32), jax.ShapeDtypeStruct((height, PANEL), F32)],
        scratch_shapes=[
            pltpu.VMEM((PANEL, DIM), F32), pltpu.VMEM((8, PANEL), F32), pltpu.VMEM((PANEL, PANEL), BF16),
            pltpu.VMEM((PANEL, PANEL), BF16), pltpu.VMEM((height, PANEL), BF16), pltpu.VMEM((height, PANEL), BF16),
            pltpu.VMEM((PANEL // 128, 2 * n, 128), F32),
        ],
        compiler_params=pltpu.CompilerParams(vmem_limit_bytes=48 << 20, dimension_semantics=("arbitrary",)),
        name="trailing_update",
    )(designs, far_designs, panel_points, weights, inverse, trailing)


NY, NX, NC = 4, 4, 2
DEVICES = NY * NX * NC


def place(y, x, core):
    return (y * NX + x) * NC + core


def pairs_of(grid_cols, moves):
    return [(a * grid_cols + c, b * grid_cols + c) for c in range(grid_cols) for a, b in moves(c)]


def gather_designs(designs, grid_cols):
    axes = ("prow", "pcol")
    at = lax.axis_index("prow")
    col = lax.axis_index("pcol")
    x_at, y_at, core = at // NC % NX, at // (NX * NC), at % NC
    cores, xs, ys = range(NC), range(NX), range(NY)
    send = lambda block, moves: lax.ppermute(block, axes, pairs_of(grid_cols, moves))

    from_x = [designs] + [
        lax.ppermute(designs, "prow", [(place(y, x, c), place(y, (x + s) % NX, c)) for y in ys for x in xs for c in cores])
        for s in range(1, NX)
    ]

    def block_of(x):
        shift = (x_at - x) % NX
        block = from_x[0]
        for s in range(1, NX):
            block = jnp.where(shift == s, from_x[s], block)
        return block

    panel = block_of(NX - 1)
    got = [send(panel, lambda _: [(place(NY - 1, x, c), place(t, x, c)) for x in xs for c in cores]) for t in range(NY - 1)]
    for t in range(NY - 1):
        panel = jnp.where(y_at == t, got[t], panel)
    other = lax.ppermute(panel, "prow", [(j, j ^ 1) for j in range(DEVICES)])
    panel_points = jnp.where(core == 0, jnp.concatenate([panel, other], 0), jnp.concatenate([other, panel], 0))

    half = 2 * (col % 2)
    far = jnp.stack([block_of(half), block_of(half + 1)], 0)
    got = [
        send(far, lambda z: [(place(z // 2, x, c), place((z // 2 + s) % NY, x, c)) for x in xs for c in cores])
        for s in range(1, NY)
    ]
    for s in range(1, NY):
        far = jnp.where((y_at - col // 2) % NY == s, got[s - 1], far)
    other = lax.ppermute(far, "prow", [(j, j ^ 1) for j in range(DEVICES)])
    first = jnp.where(core == 0, far, other)
    second = jnp.where(core == 0, other, far)
    far_designs = jnp.stack([first, second], 1).reshape(-1, DIM)
    return panel_points, far_designs


def body(designs, length_weights, trailing):
    grid_cols = lax.axis_size("pcol")
    col_index = lax.axis_index("pcol")
    weights = length_weights.reshape(1, DIM)
    panel_points, far_designs = gather_designs(designs, grid_cols)
    factor, inverse = factor_call(panel_points, weights)
    updated, rows = update_call(designs, far_designs, panel_points, weights, inverse, trailing)
    width = PANEL // grid_cols
    take = lambda whole: lax.dynamic_slice_in_dim(whole, col_index * width, width, 1)
    return updated, take(rows), take(factor)


def solution(mesh):
    in_specs = (P("prow", None), P(), P("prow", "pcol"))
    out_specs = (P("prow", "pcol"), P("prow", "pcol"), P(None, "pcol"))
    return jax.shard_map(body, mesh=mesh, in_specs=in_specs, out_specs=out_specs, check_vma=False)
```

```python
import math

import jax
import jax.numpy as jnp
from jax import lax
from jax.experimental import pallas as pl
from jax.experimental.pallas import tpu as pltpu
from jax.sharding import PartitionSpec as P

PANEL = 512
DIM = 64
BLOCK = 128
GROUP = 8

signal_variance = 4.0
nugget_level = 0.1

F32 = jnp.float32
BF16 = jnp.bfloat16
HIGHEST = lax.Precision.HIGHEST
NT = (((1,), (1,)), ((), ()))
NN = (((1,), (0,)), ((), ()))


def dot_nt(a, b):
    return lax.dot_general(a, b, NT, precision=HIGHEST, preferred_element_type=F32)


def dot_nn(a, b):
    return lax.dot_general(a, b, NN, precision=HIGHEST, preferred_element_type=F32)


def split(x):
    hi = x.astype(BF16)
    return hi, (x - hi.astype(F32)).astype(BF16)


def dot_one(a, b, dims):
    return lax.dot_general(a, b, dims, preferred_element_type=F32)


def dot_split(a, b, dims=NT):
    return dot_one(a[0], b[0], dims) + (dot_one(a[0], b[1], dims) + dot_one(a[1], b[0], dims))


def lane_take(x, lanes):
    return jnp.take_along_axis(x, lanes, axis=1, mode="promise_in_bounds")


def lane_spread(x, lane):
    return lane_take(x, jnp.full(x.shape, lane, jnp.int32))


def row_spread(x, row):
    return jnp.broadcast_to(x[row : row + 1, :], (8, 128))


def factor_block(rows):
    lane = lax.broadcasted_iota(jnp.int32, (8, 128), 1)
    sub = lax.broadcasted_iota(jnp.int32, (8, 128), 0)
    rows = list(rows)
    cols = [lane_spread(rows[0], j) for j in range(GROUP)]
    for g in range(len(rows)):
        base = GROUP * g
        slab = rows[g]
        s = [[row_spread(cols[j], k) if k <= j else None for j in range(GROUP)] for k in range(GROUP)]
        r = [None] * GROUP
        u = [[None] * GROUP for _ in range(GROUP)]
        for k in range(GROUP):
            r[k] = lax.rsqrt(s[k][k])
            for j in range(k + 1, GROUP):
                u[k][j] = s[k][j] * r[k]
            for i in range(k + 1, GROUP):
                for j in range(i, GROUP):
                    s[i][j] = s[i][j] - u[k][i] * u[k][j]
        pivots = []
        clean = []
        within = (lane >= base) & (lane < base + GROUP)
        final = slab
        for k in range(GROUP):
            row = row_spread(slab, k)
            for m in range(k):
                row = row - u[m][k] * pivots[m]
            row = row * r[k]
            diag = lane == base + k
            own = jnp.where(diag, r[k], row)
            final = jnp.where(sub == k, own, final)
            clean.append(jnp.where(within & (lane > base + k), 0.0, own))
            pivots.append(jnp.where(diag, s[k][k] * r[k] + r[k], row))
        rows[g] = final
        for i in range(g + 1, len(rows)):
            x = rows[i]
            if i == g + 1:
                c = [lane_spread(x, base + j) for j in range(GROUP)]
                cols = [lane_spread(x, base + GROUP + j) for j in range(GROUP)]
                for k in range(GROUP):
                    low = c[k] * r[k]
                    for j in range(k + 1, GROUP):
                        c[j] = c[j] - low * u[k][j]
                    cols = [cols[j] - low * row_spread(low, j) for j in range(GROUP)]
                    x = x - low * pivots[k]
            else:
                x = jnp.where(within, 0.0, x)
                for k in range(GROUP):
                    x = x - lane_take(clean[k], GROUP * i + sub) * clean[k]
            rows[i] = x
    return rows


def kernel_values(rows, points):
    squares_rows = jnp.sum(rows * rows, axis=1, keepdims=True)
    squares_points = jnp.sum(points * points, axis=0, keepdims=True)
    gaps = squares_rows + squares_points - 2.0 * dot_nn(rows, points)
    return signal_variance * jnp.exp(-gaps)


def gap_along(rows, points, d):
    return rows[:, d : d + 1] - points[d : d + 1, :]


def roots_column(roots_ref):
    return jnp.broadcast_to(roots_ref[...], (8, DIM)).T[:, 0:1]


def factor_kernel(col_ref, first_ref, second_ref, roots_ref, shard_ref, inverse_ref, factor_ref, work_ref, block_ref, turn_ref):
    points = jnp.concatenate([first_ref[...], second_ref[...]], 1) * roots_column(roots_ref)
    rows = points.T
    kernel = kernel_values(rows, points)
    gap = gap_along(rows, points, DIM - 2)
    row_iota = lax.broadcasted_iota(jnp.int32, (PANEL, PANEL), 0)
    col_iota = lax.broadcasted_iota(jnp.int32, (PANEL, PANEL), 1)
    work_ref[...] = kernel * (1.0 - 2.0 * gap * gap) + jnp.where(row_iota == col_iota, nugget_level, 0.0)
    factor_ref[...] = jnp.zeros_like(factor_ref)
    inverse_ref[...] = jnp.zeros_like(inverse_ref)

    @pl.loop(0, PANEL // BLOCK)
    def _(step):
        at = pl.multiple_of(step * BLOCK, BLOCK)
        rows = [work_ref[pl.ds(at + 8 * i, 8), pl.ds(at, BLOCK)] for i in range(BLOCK // 8)]
        rows = factor_block(rows)
        for i in range(BLOCK // 8):
            block_ref[8 * i : 8 * i + 8, :] = rows[i]
        both = block_ref[...]
        r = lax.broadcasted_iota(jnp.int32, (BLOCK, BLOCK), 0)
        c = lax.broadcasted_iota(jnp.int32, (BLOCK, BLOCK), 1)
        upper = jnp.where(c > r, both, jnp.where(c == r, 1.0 / both, 0.0))
        factor_ref[pl.ds(at, BLOCK), pl.ds(at, BLOCK)] = upper.T
        inverse = jnp.where(c <= r, both, 0.0)
        inverse_ref[pl.ds(at, BLOCK), pl.ds(at, BLOCK)] = inverse
        for s in range(PANEL // BLOCK - 1):

            @pl.when(step == s)
            def _():
                end = BLOCK * (s + 1)
                below = dot_nt(work_ref[end:, end - BLOCK : end], inverse)
                factor_ref[end:, end - BLOCK : end] = below
                work_ref[end:, end:] = work_ref[end:, end:] - dot_nt(below, below)

    for n in (BLOCK, 2 * BLOCK):
        for t in range(0, PANEL, 2 * n):
            left = dot_nn(factor_ref[t + n : t + 2 * n, t : t + n], inverse_ref[t : t + n, t : t + n])
            inverse_ref[t + n : t + 2 * n, t : t + n] = -dot_nn(
                inverse_ref[t + n : t + 2 * n, t + n : t + 2 * n], left
            )

    width = shard_ref.shape[0]
    start = col_ref[0] * width
    for s in range(PANEL // BLOCK):

        @pl.when(start // BLOCK == s)
        def _():
            turn_ref[...] = factor_ref[:, BLOCK * s : BLOCK * s + BLOCK].T
            shard_ref[...] = turn_ref[pl.ds(pl.multiple_of(start - BLOCK * s, width), width), :]


IN_SMEM = pl.BlockSpec(memory_space=pltpu.SMEM)
IN_VMEM = pl.BlockSpec(memory_space=pltpu.VMEM)


def factor_call(col, width, first, second, roots):
    return pl.pallas_call(
        factor_kernel,
        in_specs=[IN_SMEM, IN_VMEM, IN_VMEM, IN_VMEM],
        out_shape=[jax.ShapeDtypeStruct((width, PANEL), F32), jax.ShapeDtypeStruct((PANEL, PANEL), F32)],
        scratch_shapes=[
            pltpu.VMEM((PANEL, PANEL), F32), pltpu.VMEM((PANEL, PANEL), F32), pltpu.VMEM((BLOCK, BLOCK), F32),
            pltpu.VMEM((BLOCK, PANEL), F32),
        ],
        compiler_params=pltpu.CompilerParams(vmem_limit_bytes=32 << 20),
        name="panel_factor",
    )(col, first, second, roots)


def cross_rows(designs, root_weights, points, cross_ref):
    rows = (designs * root_weights).T
    kernel = kernel_values(rows, points)
    gap_u = gap_along(rows, points, DIM - 2)
    gap_v = gap_along(rows, points, DIM - 1)
    n = rows.shape[0]
    derivative = -2.0 * kernel * gap_v * gap_u
    value = math.sqrt(2.0) * kernel * gap_u
    for q in range(PANEL // 128):
        cross_ref[q, pl.ds(0, n, stride=2), :] = derivative[:, 128 * q : 128 * q + 128]
        cross_ref[q, pl.ds(1, n, stride=2), :] = value[:, 128 * q : 128 * q + 128]
    return jnp.concatenate([cross_ref[q] for q in range(PANEL // 128)], 1)


def update_kernel(
    col_ref, own_ref, first_ref, second_ref, roots_ref, inverse_ref, far_ref, trailing_ref,
    updated_ref, shard_ref, points_ref, root_ref, hi_ref, lo_ref, cross_ref, tiles_ref, sems,
):
    half = PANEL // 2
    step = pl.program_id(0)
    steps, _, tile_width = tiles_ref.shape

    def tile_copy(j):
        columns = trailing_ref.at[:, pl.ds(pl.multiple_of(j * tile_width, 128), tile_width)]
        return pltpu.make_async_copy(columns, tiles_ref.at[j], sems.at[j])

    @pl.when(step == 0)
    def _():
        for j in range(steps):
            tile_copy(j).start()
        root_ref[...] = roots_column(roots_ref)
        points_ref[...] = jnp.concatenate([first_ref[...], second_ref[...]], 1) * root_ref[...]
        cross = cross_rows(own_ref[...], root_ref[...], points_ref[...], cross_ref)
        left = dot_nt(cross[:, :half], inverse_ref[:half, :half])
        right = dot_nt(cross, inverse_ref[half:, :])
        left_hi, left_lo = split(left)
        right_hi, right_lo = split(right)
        rows_hi = jnp.concatenate([left_hi, right_hi], 1)
        rows_lo = jnp.concatenate([left_lo, right_lo], 1)
        width = shard_ref.shape[0]
        chosen = lax.broadcasted_iota(jnp.int32, (width, PANEL), 0) + col_ref[0] * width
        pick = jnp.where(lax.broadcasted_iota(jnp.int32, (width, PANEL), 1) == chosen, 1.0, 0.0).astype(BF16)
        shard_ref[...] = dot_one(pick, rows_hi, NT) + dot_one(pick, rows_lo, NT)
        inv_hi, inv_lo = split(inverse_ref[...])
        left = dot_split((rows_hi, rows_lo), (inv_hi[:, :half], inv_lo[:, :half]), NN)
        right = dot_split((right_hi, right_lo), (inv_hi[half:, half:], inv_lo[half:, half:]), NN)
        hi_ref[:, :half], lo_ref[:, :half] = split(left)
        hi_ref[:, half:], lo_ref[:, half:] = split(right)

    far = split(cross_rows(far_ref[0], root_ref[...], points_ref[...], cross_ref))
    product = dot_split((hi_ref[...], lo_ref[...]), far)
    tile_copy(step).wait()
    updated_ref[...] = tiles_ref[step] - product


def update_call(col, panel_width, own, first, second, roots, inverse, far, trailing):
    n = own.shape[1]
    height, width = trailing.shape
    steps = far.shape[0]
    tile = pl.BlockSpec((height, width // steps), lambda j: (0, j))
    return pl.pallas_call(
        update_kernel,
        grid=(steps,),
        in_specs=[
            IN_SMEM, IN_VMEM, IN_VMEM, IN_VMEM, IN_VMEM, IN_VMEM, pl.BlockSpec((1, DIM, n), lambda j: (j, 0, 0)),
            pl.BlockSpec(memory_space=pltpu.HBM),
        ],
        out_specs=[tile, pl.BlockSpec((panel_width, height), lambda j: (0, 0))],
        out_shape=[jax.ShapeDtypeStruct((height, width), F32), jax.ShapeDtypeStruct((panel_width, height), F32)],
        scratch_shapes=[
            pltpu.VMEM((DIM, PANEL), F32), pltpu.VMEM((DIM, 1), F32), pltpu.VMEM((height, PANEL), BF16),
            pltpu.VMEM((height, PANEL), BF16), pltpu.VMEM((PANEL // 128, 2 * n, 128), F32),
            pltpu.VMEM((steps, height, width // steps), F32), pltpu.SemaphoreType.DMA((steps,)),
        ],
        compiler_params=pltpu.CompilerParams(vmem_limit_bytes=48 << 20, dimension_semantics=("arbitrary",)),
        name="trailing_update",
    )(col, own, first, second, roots, inverse, far, pltpu.with_memory_space_constraint(trailing, pltpu.HBM))


NY, NX, NC = 4, 4, 2
DEVICES = NY * NX * NC


def place(y, x, core):
    return (y * NX + x) * NC + core


def gather_designs(designs, roots):
    at = lax.axis_index("prow")
    col = lax.axis_index("pcol")
    x_at, y_at, core = at // NC % NX, at // (NX * NC), at % NC
    cores, xs, ys = range(NC), range(NX), range(NY)
    along_x = [[(place(y, x, c), place(y, (x + s) % NX, c)) for y in ys for x in xs for c in cores] for s in range(NX)]
    along_y = [[(place(y, x, c), place((y + s) % NY, x, c)) for y in ys for x in xs for c in cores] for s in range(NY)]
    swap = [(j, j ^ 1) for j in range(DEVICES)]
    send = lambda block, pairs: lax.ppermute(block, "prow", pairs)

    def rounds(block, pairs):
        got = {s: send(block, pairs[s]) for s in (2, 1, 3)}
        return [block] + [got[s] for s in (1, 2, 3)]

    def pick(blocks, shift):
        chosen = blocks[0]
        for s in range(1, len(blocks)):
            chosen = jnp.where(shift == s, blocks[s], chosen)
        return chosen

    from_x = rounds(designs, along_x)
    block_of = lambda x: pick(from_x, (x_at - x) % NX)
    panel, roots = lax.optimization_barrier((block_of(NX - 1), roots))
    panel = pick(rounds(panel, along_y), (y_at - (NY - 1)) % NY)
    half = 2 * (col % 2)
    far = jnp.stack([block_of(half), block_of(half + 1)], 0)
    far_other = send(far, swap)
    other = send(panel, swap)
    first = jnp.where(core == 0, panel, other)
    second = jnp.where(core == 0, other, panel)
    far = jnp.stack([jnp.where(core == 0, far, far_other), jnp.where(core == 0, far_other, far)], 1)
    far = far.reshape(2 * NC, *designs.shape)
    first, second, far = lax.optimization_barrier((first, second, far))
    far = pick(rounds(far, along_y), (y_at - col // 2) % NY)
    return first, second, far, roots


def body(designs, length_weights, trailing):
    width = PANEL // lax.axis_size("pcol")
    col = lax.axis_index("pcol").reshape(1)
    own = designs.T
    first, second, far, roots = gather_designs(own, jnp.sqrt(length_weights).reshape(1, DIM))
    factor_shard, inverse = factor_call(col, width, first, second, roots)
    updated, rows_shard = update_call(col, width, own, first, second, roots, inverse, far, trailing)
    return updated, rows_shard.T, factor_shard.T


def solution(mesh):
    in_specs = (P("prow", None), P(), P("prow", "pcol"))
    out_specs = (P("prow", "pcol"), P("prow", "pcol"), P(None, "pcol"))
    return jax.shard_map(body, mesh=mesh, in_specs=in_specs, out_specs=out_specs, check_vma=False)
```

```python
import math

import jax
import jax.numpy as jnp
from jax import lax
from jax.experimental import pallas as pl
from jax.experimental.pallas import tpu as pltpu
from jax.sharding import PartitionSpec as P

PANEL = 512
DIM = 64
BLOCK = 128
GROUP = 8

signal_variance = 4.0
nugget_level = 0.1

F32 = jnp.float32
BF16 = jnp.bfloat16
HIGHEST = lax.Precision.HIGHEST
NT = (((1,), (1,)), ((), ()))
NN = (((1,), (0,)), ((), ()))
TN = (((0,), (0,)), ((), ()))


def dot_nt(a, b):
    return lax.dot_general(a, b, NT, precision=HIGHEST, preferred_element_type=F32)


def dot_nn(a, b):
    return lax.dot_general(a, b, NN, precision=HIGHEST, preferred_element_type=F32)


def split(x):
    hi = x.astype(BF16)
    return hi, (x - hi.astype(F32)).astype(BF16)


def dot_one(a, b, dims):
    return lax.dot_general(a, b, dims, preferred_element_type=F32)


def dot_split(a, b, dims=NT):
    return dot_one(a[0], b[0], dims) + (dot_one(a[0], b[1], dims) + dot_one(a[1], b[0], dims))


def lane_take(x, lanes):
    return jnp.take_along_axis(x, lanes, axis=1, mode="promise_in_bounds")


def lane_spread(x, lane):
    return lane_take(x, jnp.full(x.shape, lane, jnp.int32))


def row_spread(x, row):
    return jnp.broadcast_to(x[row : row + 1, :], (8, 128))


def factor_block(rows):
    lane = lax.broadcasted_iota(jnp.int32, (8, 128), 1)
    sub = lax.broadcasted_iota(jnp.int32, (8, 128), 0)
    rows = list(rows)
    cols = [lane_spread(rows[0], j) for j in range(GROUP)]
    for g in range(len(rows)):
        base = GROUP * g
        slab = rows[g]
        s = [[row_spread(cols[j], k) if k <= j else None for j in range(GROUP)] for k in range(GROUP)]
        r = [None] * GROUP
        u = [[None] * GROUP for _ in range(GROUP)]
        for k in range(GROUP):
            r[k] = lax.rsqrt(s[k][k])
            for j in range(k + 1, GROUP):
                u[k][j] = s[k][j] * r[k]
            for i in range(k + 1, GROUP):
                for j in range(i, GROUP):
                    s[i][j] = s[i][j] - u[k][i] * u[k][j]
        pivots = []
        clean = []
        within = (lane >= base) & (lane < base + GROUP)
        final = slab
        for k in range(GROUP):
            row = row_spread(slab, k)
            for m in range(k):
                row = row - u[m][k] * pivots[m]
            row = row * r[k]
            diag = lane == base + k
            own = jnp.where(diag, r[k], row)
            final = jnp.where(sub == k, own, final)
            clean.append(jnp.where(within & (lane > base + k), 0.0, own))
            pivots.append(jnp.where(diag, s[k][k] * r[k] + r[k], row))
        rows[g] = final
        for i in range(g + 1, len(rows)):
            x = rows[i]
            if i == g + 1:
                c = [lane_spread(x, base + j) for j in range(GROUP)]
                cols = [lane_spread(x, base + GROUP + j) for j in range(GROUP)]
                for k in range(GROUP):
                    low = c[k] * r[k]
                    for j in range(k + 1, GROUP):
                        c[j] = c[j] - low * u[k][j]
                    cols = [cols[j] - low * row_spread(low, j) for j in range(GROUP)]
                    x = x - low * pivots[k]
            else:
                x = jnp.where(within, 0.0, x)
                for k in range(GROUP):
                    x = x - lane_take(clean[k], GROUP * i + sub) * clean[k]
            rows[i] = x
    return rows


def thirds(x):
    first = x.astype(BF16)
    rest = x - first.astype(F32)
    second = rest.astype(BF16)
    return first, second, (rest - second.astype(F32)).astype(BF16)


def stack_left(x):
    a, b, c = thirds(x)
    return jnp.concatenate([a, a, b, b, a, c], 0)


def stack_right(x):
    a, b, c = thirds(x)
    return jnp.concatenate([a, b, a, b, c, a], 0)


def kernel_values(scaled, points, stacked_points):
    rows = scaled.T
    squares_rows = jnp.sum(rows * rows, axis=1, keepdims=True)
    squares_points = jnp.sum(points * points, axis=0, keepdims=True)
    inner = dot_one(stack_left(scaled), stacked_points, TN)
    return rows, signal_variance * jnp.exp(-(squares_rows + squares_points - 2.0 * inner))


def gap_along(rows, points, d):
    return rows[:, d : d + 1] - points[d : d + 1, :]


def roots_column(roots_ref):
    return jnp.broadcast_to(roots_ref[...], (8, DIM)).T[:, 0:1]


def factor_kernel(col_ref, first_ref, second_ref, roots_ref, shard_ref, inverse_ref, factor_ref, work_ref, block_ref, turn_ref):
    points = jnp.concatenate([first_ref[...], second_ref[...]], 1) * roots_column(roots_ref)
    rows, kernel = kernel_values(points, points, stack_right(points))
    gap = gap_along(rows, points, DIM - 2)
    row_iota = lax.broadcasted_iota(jnp.int32, (PANEL, PANEL), 0)
    col_iota = lax.broadcasted_iota(jnp.int32, (PANEL, PANEL), 1)
    work_ref[...] = kernel * (1.0 - 2.0 * gap * gap) + jnp.where(row_iota == col_iota, nugget_level, 0.0)
    factor_ref[...] = jnp.zeros_like(factor_ref)
    inverse_ref[...] = jnp.zeros_like(inverse_ref)

    @pl.loop(0, PANEL // BLOCK)
    def _(step):
        at = pl.multiple_of(step * BLOCK, BLOCK)
        rows = [work_ref[pl.ds(at + 8 * i, 8), pl.ds(at, BLOCK)] for i in range(BLOCK // 8)]
        rows = factor_block(rows)
        for i in range(BLOCK // 8):
            block_ref[8 * i : 8 * i + 8, :] = rows[i]
        both = block_ref[...]
        r = lax.broadcasted_iota(jnp.int32, (BLOCK, BLOCK), 0)
        c = lax.broadcasted_iota(jnp.int32, (BLOCK, BLOCK), 1)
        upper = jnp.where(c > r, both, jnp.where(c == r, 1.0 / both, 0.0))
        factor_ref[pl.ds(at, BLOCK), pl.ds(at, BLOCK)] = upper.T
        inverse = jnp.where(c <= r, both, 0.0)
        inverse_ref[pl.ds(at, BLOCK), pl.ds(at, BLOCK)] = inverse
        for s in range(PANEL // BLOCK - 1):

            @pl.when(step == s)
            def _():
                end = BLOCK * (s + 1)
                below = dot_nt(work_ref[end:, end - BLOCK : end], inverse)
                factor_ref[end:, end - BLOCK : end] = below
                work_ref[end:, end:] = work_ref[end:, end:] - dot_nt(below, below)

    for n in (BLOCK, 2 * BLOCK):
        for t in range(0, PANEL, 2 * n):
            left = dot_nn(factor_ref[t + n : t + 2 * n, t : t + n], inverse_ref[t : t + n, t : t + n])
            inverse_ref[t + n : t + 2 * n, t : t + n] = -dot_nn(
                inverse_ref[t + n : t + 2 * n, t + n : t + 2 * n], left
            )

    width = shard_ref.shape[0]
    start = col_ref[0] * width
    for s in range(PANEL // BLOCK):

        @pl.when(start // BLOCK == s)
        def _():
            turn_ref[...] = factor_ref[:, BLOCK * s : BLOCK * s + BLOCK].T
            shard_ref[...] = turn_ref[pl.ds(pl.multiple_of(start - BLOCK * s, width), width), :]


IN_SMEM = pl.BlockSpec(memory_space=pltpu.SMEM)
IN_VMEM = pl.BlockSpec(memory_space=pltpu.VMEM)


def factor_call(col, width, first, second, roots):
    return pl.pallas_call(
        factor_kernel,
        in_specs=[IN_SMEM, IN_VMEM, IN_VMEM, IN_VMEM],
        out_shape=[jax.ShapeDtypeStruct((width, PANEL), F32), jax.ShapeDtypeStruct((PANEL, PANEL), F32)],
        scratch_shapes=[
            pltpu.VMEM((PANEL, PANEL), F32), pltpu.VMEM((PANEL, PANEL), F32), pltpu.VMEM((BLOCK, BLOCK), F32),
            pltpu.VMEM((BLOCK, PANEL), F32),
        ],
        compiler_params=pltpu.CompilerParams(vmem_limit_bytes=32 << 20),
        name="panel_factor",
    )(col, first, second, roots)


def cross_rows(designs, root_weights, points, stacked_points, cross_ref):
    rows, kernel = kernel_values(designs * root_weights, points, stacked_points)
    gap_u = gap_along(rows, points, DIM - 2)
    gap_v = gap_along(rows, points, DIM - 1)
    n = rows.shape[0]
    derivative = -2.0 * kernel * gap_v * gap_u
    value = math.sqrt(2.0) * kernel * gap_u
    for q in range(PANEL // 128):
        cross_ref[q, pl.ds(0, n, stride=2), :] = derivative[:, 128 * q : 128 * q + 128]
        cross_ref[q, pl.ds(1, n, stride=2), :] = value[:, 128 * q : 128 * q + 128]
    return jnp.concatenate([cross_ref[q] for q in range(PANEL // 128)], 1)


def update_kernel(
    col_ref, own_ref, first_ref, second_ref, roots_ref, inverse_ref, far_ref, trailing_ref,
    updated_ref, shard_ref, tiles_ref, cross_ref, in_sems, out_sems,
):
    half = PANEL // 2
    steps, _, tile_width = tiles_ref.shape

    def columns(ref, j):
        return ref.at[:, j * tile_width : (j + 1) * tile_width]

    arrive = [pltpu.make_async_copy(columns(trailing_ref, j), tiles_ref.at[j], in_sems.at[j]) for j in range(steps)]
    leave = [pltpu.make_async_copy(tiles_ref.at[j], columns(updated_ref, j), out_sems.at[j]) for j in range(steps)]
    for copy in arrive:
        copy.start()

    roots = roots_column(roots_ref)
    points = jnp.concatenate([first_ref[...], second_ref[...]], 1) * roots
    stacked = stack_right(points)
    cross = cross_rows(own_ref[...], roots, points, stacked, cross_ref.at[steps])
    left = dot_nt(cross[:, :half], inverse_ref[:half, :half])
    right = dot_nt(cross, inverse_ref[half:, :])
    left_hi, left_lo = split(left)
    right_hi, right_lo = split(right)
    rows_hi = jnp.concatenate([left_hi, right_hi], 1)
    rows_lo = jnp.concatenate([left_lo, right_lo], 1)
    width = shard_ref.shape[0]
    chosen = lax.broadcasted_iota(jnp.int32, (width, PANEL), 0) + col_ref[0] * width
    pick = jnp.where(lax.broadcasted_iota(jnp.int32, (width, PANEL), 1) == chosen, 1.0, 0.0).astype(BF16)
    shard_ref[...] = dot_one(pick, rows_hi, NT) + dot_one(pick, rows_lo, NT)
    inv_hi, inv_lo = split(inverse_ref[...])
    left = dot_split((rows_hi, rows_lo), (inv_hi[:, :half], inv_lo[:, :half]), NN)
    right = dot_split((right_hi, right_lo), (inv_hi[half:, half:], inv_lo[half:, half:]), NN)
    left_hi, left_lo = split(left)
    right_hi, right_lo = split(right)
    rows = (jnp.concatenate([left_hi, right_hi], 1), jnp.concatenate([left_lo, right_lo], 1))

    far = split(cross_rows(far_ref[0], roots, points, stacked, cross_ref.at[0]))
    for copy in arrive:
        copy.wait()
    for j in range(steps):
        here = far
        if j + 1 < steps:
            far = split(cross_rows(far_ref[j + 1], roots, points, stacked, cross_ref.at[j + 1]))
        tiles_ref[j] = tiles_ref[j] - dot_split(rows, here)
        leave[j].start()
    for copy in leave:
        copy.wait()


def update_call(col, panel_width, own, first, second, roots, inverse, far, trailing):
    n = own.shape[1]
    height, width = trailing.shape
    steps = far.shape[0]
    in_hbm = pl.BlockSpec(memory_space=pltpu.HBM)
    return pl.pallas_call(
        update_kernel,
        in_specs=[IN_SMEM] + [IN_VMEM] * 6 + [in_hbm],
        out_specs=[in_hbm, IN_VMEM],
        out_shape=[jax.ShapeDtypeStruct((height, width), F32), jax.ShapeDtypeStruct((panel_width, height), F32)],
        scratch_shapes=[
            pltpu.VMEM((steps, height, width // steps), F32), pltpu.VMEM((steps + 1, PANEL // 128, 2 * n, 128), F32),
            pltpu.SemaphoreType.DMA((steps,)), pltpu.SemaphoreType.DMA((steps,)),
        ],
        compiler_params=pltpu.CompilerParams(vmem_limit_bytes=40 << 20),
        name="trailing_update",
    )(col, own, first, second, roots, inverse, far, pltpu.with_memory_space_constraint(trailing, pltpu.HBM))


NY, NX, NC = 4, 4, 2
DEVICES = NY * NX * NC


def place(y, x, core):
    return (y * NX + x) * NC + core


def gather_designs(designs, roots):
    at = lax.axis_index("prow")
    col = lax.axis_index("pcol")
    x_at, y_at, core = at // NC % NX, at // (NX * NC), at % NC
    cores, xs, ys = range(NC), range(NX), range(NY)
    along_x = [[(place(y, x, c), place(y, (x + s) % NX, c)) for y in ys for x in xs for c in cores] for s in range(NX)]
    along_y = [[(place(y, x, c), place((y + s) % NY, x, c)) for y in ys for x in xs for c in cores] for s in range(NY)]
    swap = [(j, j ^ 1) for j in range(DEVICES)]
    send = lambda block, pairs: lax.ppermute(block, "prow", pairs)

    def rounds(block, pairs):
        got = {s: send(block, pairs[s]) for s in (2, 1, 3)}
        return [block] + [got[s] for s in (1, 2, 3)]

    def pick(blocks, shift):
        chosen = blocks[0]
        for s in range(1, len(blocks)):
            chosen = jnp.where(shift == s, blocks[s], chosen)
        return chosen

    from_x = rounds(designs, along_x)
    one = jnp.where(at >= 0, 1.0, 2.0).astype(F32)
    from_x[0] = lax.optimization_barrier(designs * one)
    block_of = lambda x: pick(from_x, (x_at - x) % NX)
    panel, roots = lax.optimization_barrier((block_of(NX - 1), roots))
    panel = pick(rounds(panel, along_y), (y_at - (NY - 1)) % NY)
    half = 2 * (col % 2)
    far = jnp.stack([block_of(half), block_of(half + 1)], 0)
    far_other = send(far, swap)
    other = send(panel, swap)
    first = jnp.where(core == 0, panel, other)
    second = jnp.where(core == 0, other, panel)
    far = jnp.stack([jnp.where(core == 0, far, far_other), jnp.where(core == 0, far_other, far)], 1)
    far = far.reshape(2 * NC, *designs.shape)
    first, second, far = lax.optimization_barrier((first, second, far))
    far = pick(rounds(far, along_y), (y_at - col // 2) % NY)
    return from_x[0], first, second, far, roots


def body(designs, length_weights, trailing):
    width = PANEL // lax.axis_size("pcol")
    col = lax.axis_index("pcol").reshape(1)
    own, first, second, far, roots = gather_designs(designs.T, jnp.sqrt(length_weights).reshape(1, DIM))
    factor_shard, inverse = factor_call(col, width, first, second, roots)
    updated, rows_shard = update_call(col, width, own, first, second, roots, inverse, far, trailing)
    return updated, rows_shard.T, factor_shard.T


def solution(mesh):
    in_specs = (P("prow", None), P(), P("prow", "pcol"))
    out_specs = (P("prow", "pcol"), P("prow", "pcol"), P(None, "pcol"))
    return jax.shard_map(body, mesh=mesh, in_specs=in_specs, out_specs=out_specs, check_vma=False)
```

```python
import math

import jax
import jax.numpy as jnp
from jax import lax
from jax.experimental import pallas as pl
from jax.experimental.pallas import tpu as pltpu
from jax.sharding import PartitionSpec as P

PANEL = 512
DIM = 64
BLOCK = 128
GROUP = 8

signal_variance = 4.0
nugget_level = 0.1

F32 = jnp.float32
BF16 = jnp.bfloat16
HIGHEST = lax.Precision.HIGHEST
NT = (((1,), (1,)), ((), ()))
NN = (((1,), (0,)), ((), ()))
TN = (((0,), (0,)), ((), ()))


def dot_nt(a, b):
    return lax.dot_general(a, b, NT, precision=HIGHEST, preferred_element_type=F32)


def dot_nn(a, b):
    return lax.dot_general(a, b, NN, precision=HIGHEST, preferred_element_type=F32)


def split(x):
    hi = x.astype(BF16)
    return hi, (x - hi.astype(F32)).astype(BF16)


def dot_one(a, b, dims):
    return lax.dot_general(a, b, dims, preferred_element_type=F32)


def dot_split(a, b, dims=NT):
    return dot_one(a[0], b[0], dims) + (dot_one(a[0], b[1], dims) + dot_one(a[1], b[0], dims))


def lane_take(x, lanes):
    return jnp.take_along_axis(x, lanes, axis=1, mode="promise_in_bounds")


def lane_spread(x, lane):
    return lane_take(x, jnp.full(x.shape, lane, jnp.int32))


def row_spread(x, row):
    return jnp.broadcast_to(x[row : row + 1, :], (8, 128))


def factor_block(rows):
    lane = lax.broadcasted_iota(jnp.int32, (8, 128), 1)
    sub = lax.broadcasted_iota(jnp.int32, (8, 128), 0)
    rows = list(rows)
    cols = [lane_spread(rows[0], j) for j in range(GROUP)]
    for g in range(len(rows)):
        base = GROUP * g
        slab = rows[g]
        s = [[row_spread(cols[j], k) if k <= j else None for j in range(GROUP)] for k in range(GROUP)]
        r = [None] * GROUP
        u = [[None] * GROUP for _ in range(GROUP)]
        for k in range(GROUP):
            r[k] = lax.rsqrt(s[k][k])
            for j in range(k + 1, GROUP):
                u[k][j] = s[k][j] * r[k]
            for i in range(k + 1, GROUP):
                for j in range(i, GROUP):
                    s[i][j] = s[i][j] - u[k][i] * u[k][j]
        pivots = []
        clean = []
        within = (lane >= base) & (lane < base + GROUP)
        final = slab
        for k in range(GROUP):
            row = row_spread(slab, k)
            for m in range(k):
                row = row - u[m][k] * pivots[m]
            row = row * r[k]
            diag = lane == base + k
            own = jnp.where(diag, r[k], row)
            final = jnp.where(sub == k, own, final)
            clean.append(jnp.where(within & (lane > base + k), 0.0, own))
            pivots.append(jnp.where(diag, s[k][k] * r[k] + r[k], row))
        rows[g] = final
        for i in range(g + 1, len(rows)):
            x = rows[i]
            if i == g + 1:
                c = [lane_spread(x, base + j) for j in range(GROUP)]
                cols = [lane_spread(x, base + GROUP + j) for j in range(GROUP)]
                for k in range(GROUP):
                    low = c[k] * r[k]
                    for j in range(k + 1, GROUP):
                        c[j] = c[j] - low * u[k][j]
                    cols = [cols[j] - low * row_spread(low, j) for j in range(GROUP)]
                    x = x - low * pivots[k]
            else:
                x = jnp.where(within, 0.0, x)
                for k in range(GROUP):
                    x = x - lane_take(clean[k], GROUP * i + sub) * clean[k]
            rows[i] = x
    return rows


def thirds(x):
    first = x.astype(BF16)
    rest = x - first.astype(F32)
    second = rest.astype(BF16)
    return first, second, (rest - second.astype(F32)).astype(BF16)


def stack_left(x):
    a, b, c = thirds(x)
    return jnp.concatenate([a, a, b, b, a, c], 0)


def stack_right(x):
    a, b, c = thirds(x)
    return jnp.concatenate([a, b, a, b, c, a], 0)


def kernel_values(scaled, points, stacked_points):
    rows = scaled.T
    squares_rows = jnp.sum(rows * rows, axis=1, keepdims=True)
    squares_points = jnp.sum(points * points, axis=0, keepdims=True)
    inner = dot_one(stack_left(scaled), stacked_points, TN)
    return rows, signal_variance * jnp.exp(-(squares_rows + squares_points - 2.0 * inner))


def gap_along(rows, points, d):
    return rows[:, d : d + 1] - points[d : d + 1, :]


def roots_column(roots_ref):
    return jnp.broadcast_to(roots_ref[...], (8, DIM)).T[:, 0:1]


def factor_kernel(col_ref, first_ref, second_ref, roots_ref, shard_ref, inverse_ref, factor_ref, work_ref, block_ref, turn_ref):
    points = jnp.concatenate([first_ref[...], second_ref[...]], 1) * roots_column(roots_ref)
    rows, kernel = kernel_values(points, points, stack_right(points))
    gap = gap_along(rows, points, DIM - 2)
    row_iota = lax.broadcasted_iota(jnp.int32, (PANEL, PANEL), 0)
    col_iota = lax.broadcasted_iota(jnp.int32, (PANEL, PANEL), 1)
    work_ref[...] = kernel * (1.0 - 2.0 * gap * gap) + jnp.where(row_iota == col_iota, nugget_level, 0.0)
    factor_ref[...] = jnp.zeros_like(factor_ref)
    inverse_ref[...] = jnp.zeros_like(inverse_ref)

    @pl.loop(0, PANEL // BLOCK)
    def _(step):
        at = pl.multiple_of(step * BLOCK, BLOCK)
        rows = [work_ref[pl.ds(at + 8 * i, 8), pl.ds(at, BLOCK)] for i in range(BLOCK // 8)]
        rows = factor_block(rows)
        for i in range(BLOCK // 8):
            block_ref[8 * i : 8 * i + 8, :] = rows[i]
        both = block_ref[...]
        r = lax.broadcasted_iota(jnp.int32, (BLOCK, BLOCK), 0)
        c = lax.broadcasted_iota(jnp.int32, (BLOCK, BLOCK), 1)
        upper = jnp.where(c > r, both, jnp.where(c == r, 1.0 / both, 0.0))
        factor_ref[pl.ds(at, BLOCK), pl.ds(at, BLOCK)] = upper.T
        inverse = jnp.where(c <= r, both, 0.0)
        inverse_ref[pl.ds(at, BLOCK), pl.ds(at, BLOCK)] = inverse
        for s in range(PANEL // BLOCK - 1):

            @pl.when(step == s)
            def _():
                end = BLOCK * (s + 1)
                below = dot_nt(work_ref[end:, end - BLOCK : end], inverse)
                factor_ref[end:, end - BLOCK : end] = below
                for t in range(0, PANEL - end, BLOCK):
                    top = end + t
                    product = dot_nt(below[t:], below[t : t + BLOCK])
                    work_ref[top:, top : top + BLOCK] = work_ref[top:, top : top + BLOCK] - product

    for n in (BLOCK, 2 * BLOCK):
        for t in range(0, PANEL, 2 * n):
            left = dot_nn(factor_ref[t + n : t + 2 * n, t : t + n], inverse_ref[t : t + n, t : t + n])
            inverse_ref[t + n : t + 2 * n, t : t + n] = -dot_nn(
                inverse_ref[t + n : t + 2 * n, t + n : t + 2 * n], left
            )

    width = shard_ref.shape[0]
    start = col_ref[0] * width
    for s in range(PANEL // BLOCK):

        @pl.when(start // BLOCK == s)
        def _():
            turn_ref[...] = factor_ref[:, BLOCK * s : BLOCK * s + BLOCK].T
            shard_ref[...] = turn_ref[pl.ds(pl.multiple_of(start - BLOCK * s, width), width), :]


IN_SMEM = pl.BlockSpec(memory_space=pltpu.SMEM)
IN_VMEM = pl.BlockSpec(memory_space=pltpu.VMEM)


def factor_call(col, width, first, second, roots):
    return pl.pallas_call(
        factor_kernel,
        in_specs=[IN_SMEM, IN_VMEM, IN_VMEM, IN_VMEM],
        out_shape=[jax.ShapeDtypeStruct((width, PANEL), F32), jax.ShapeDtypeStruct((PANEL, PANEL), F32)],
        scratch_shapes=[
            pltpu.VMEM((PANEL, PANEL), F32), pltpu.VMEM((PANEL, PANEL), F32), pltpu.VMEM((BLOCK, BLOCK), F32),
            pltpu.VMEM((BLOCK, PANEL), F32),
        ],
        compiler_params=pltpu.CompilerParams(vmem_limit_bytes=32 << 20),
        name="panel_factor",
    )(col, first, second, roots)


def cross_rows(designs, root_weights, points, stacked_points, cross_ref):
    rows, kernel = kernel_values(designs * root_weights, points, stacked_points)
    gap_u = gap_along(rows, points, DIM - 2)
    gap_v = gap_along(rows, points, DIM - 1)
    n = rows.shape[0]
    derivative = -2.0 * kernel * gap_v * gap_u
    value = math.sqrt(2.0) * kernel * gap_u
    for q in range(PANEL // 128):
        cross_ref[q, pl.ds(0, n, stride=2), :] = derivative[:, 128 * q : 128 * q + 128]
        cross_ref[q, pl.ds(1, n, stride=2), :] = value[:, 128 * q : 128 * q + 128]
    return jnp.concatenate([cross_ref[q] for q in range(PANEL // 128)], 1)


def update_kernel(
    col_ref, own_ref, first_ref, second_ref, roots_ref, inverse_ref, far_ref, trailing_ref,
    updated_ref, shard_ref, tiles_ref, cross_ref, in_sems, out_sems,
):
    half = PANEL // 2
    steps, _, tile_width = tiles_ref.shape

    def columns(ref, j):
        return ref.at[:, j * tile_width : (j + 1) * tile_width]

    arrive = [pltpu.make_async_copy(columns(trailing_ref, j), tiles_ref.at[j], in_sems.at[j]) for j in range(steps)]
    leave = [pltpu.make_async_copy(tiles_ref.at[j], columns(updated_ref, j), out_sems.at[j]) for j in range(steps)]
    for copy in arrive:
        copy.start()

    roots = roots_column(roots_ref)
    points = jnp.concatenate([first_ref[...], second_ref[...]], 1) * roots
    stacked = stack_right(points)
    cross = cross_rows(own_ref[...], roots, points, stacked, cross_ref.at[steps])
    left = dot_nt(cross[:, :half], inverse_ref[:half, :half])
    right = dot_nt(cross, inverse_ref[half:, :])
    left_hi, left_lo = split(left)
    right_hi, right_lo = split(right)
    rows_hi = jnp.concatenate([left_hi, right_hi], 1)
    rows_lo = jnp.concatenate([left_lo, right_lo], 1)
    width = shard_ref.shape[0]
    chosen = lax.broadcasted_iota(jnp.int32, (width, PANEL), 0) + col_ref[0] * width
    pick = jnp.where(lax.broadcasted_iota(jnp.int32, (width, PANEL), 1) == chosen, 1.0, 0.0).astype(BF16)
    shard_ref[...] = dot_one(pick, rows_hi, NT) + dot_one(pick, rows_lo, NT)
    inv_hi, inv_lo = split(inverse_ref[...])
    left = dot_split((rows_hi, rows_lo), (inv_hi[:, :half], inv_lo[:, :half]), NN)
    right = dot_split((right_hi, right_lo), (inv_hi[half:, half:], inv_lo[half:, half:]), NN)
    left_hi, left_lo = split(left)
    right_hi, right_lo = split(right)
    rows = (jnp.concatenate([left_hi, right_hi], 1), jnp.concatenate([left_lo, right_lo], 1))

    far = split(cross_rows(far_ref[0], roots, points, stacked, cross_ref.at[0]))
    for copy in arrive:
        copy.wait()
    for j in range(steps):
        here = far
        if j + 1 < steps:
            far = split(cross_rows(far_ref[j + 1], roots, points, stacked, cross_ref.at[j + 1]))
        tiles_ref[j] = tiles_ref[j] - dot_split(rows, here)
        leave[j].start()
    for copy in leave:
        copy.wait()


def update_call(col, panel_width, own, first, second, roots, inverse, far, trailing):
    n = own.shape[1]
    height, width = trailing.shape
    steps = far.shape[0]
    in_hbm = pl.BlockSpec(memory_space=pltpu.HBM)
    return pl.pallas_call(
        update_kernel,
        in_specs=[IN_SMEM] + [IN_VMEM] * 6 + [in_hbm],
        out_specs=[in_hbm, IN_VMEM],
        out_shape=[jax.ShapeDtypeStruct((height, width), F32), jax.ShapeDtypeStruct((panel_width, height), F32)],
        scratch_shapes=[
            pltpu.VMEM((steps, height, width // steps), F32), pltpu.VMEM((steps + 1, PANEL // 128, 2 * n, 128), F32),
            pltpu.SemaphoreType.DMA((steps,)), pltpu.SemaphoreType.DMA((steps,)),
        ],
        compiler_params=pltpu.CompilerParams(vmem_limit_bytes=40 << 20),
        name="trailing_update",
    )(col, own, first, second, roots, inverse, far, pltpu.with_memory_space_constraint(trailing, pltpu.HBM))


NY, NX, NC = 4, 4, 2
DEVICES = NY * NX * NC


def place(y, x, core):
    return (y * NX + x) * NC + core


def gather_designs(designs, roots):
    at = lax.axis_index("prow")
    col = lax.axis_index("pcol")
    x_at, y_at, core = at // NC % NX, at // (NX * NC), at % NC
    cores, xs, ys = range(NC), range(NX), range(NY)
    along_x = [[(place(y, x, c), place(y, (x + s) % NX, c)) for y in ys for x in xs for c in cores] for s in range(NX)]
    along_y = [[(place(y, x, c), place((y + s) % NY, x, c)) for y in ys for x in xs for c in cores] for s in range(NY)]
    swap = [(j, j ^ 1) for j in range(DEVICES)]
    send = lambda block, pairs: lax.ppermute(block, "prow", pairs)

    def rounds(block, pairs):
        got = {s: send(block, pairs[s]) for s in (2, 1, 3)}
        return [block] + [got[s] for s in (1, 2, 3)]

    def pick(blocks, shift):
        chosen = blocks[0]
        for s in range(1, len(blocks)):
            chosen = jnp.where(shift == s, blocks[s], chosen)
        return chosen

    from_x = rounds(designs, along_x)
    one = jnp.where(at >= 0, 1.0, 2.0).astype(F32)
    from_x[0] = lax.optimization_barrier(designs * one)
    block_of = lambda x: pick(from_x, (x_at - x) % NX)
    panel, roots = lax.optimization_barrier((block_of(NX - 1), roots))
    panel = pick(rounds(panel, along_y), (y_at - (NY - 1)) % NY)
    half = 2 * (col % 2)
    far = jnp.stack([block_of(half), block_of(half + 1)], 0)
    far_other = send(far, swap)
    other = send(panel, swap)
    first = jnp.where(core == 0, panel, other)
    second = jnp.where(core == 0, other, panel)
    far = jnp.stack([jnp.where(core == 0, far, far_other), jnp.where(core == 0, far_other, far)], 1)
    far = far.reshape(2 * NC, *designs.shape)
    first, second, far = lax.optimization_barrier((first, second, far))
    far = pick(rounds(far, along_y), (y_at - col // 2) % NY)
    return from_x[0], first, second, far, roots


def body(designs, length_weights, trailing):
    width = PANEL // lax.axis_size("pcol")
    col = lax.axis_index("pcol").reshape(1)
    own, first, second, far, roots = gather_designs(designs.T, jnp.sqrt(length_weights).reshape(1, DIM))
    factor_shard, inverse = factor_call(col, width, first, second, roots)
    updated, rows_shard = update_call(col, width, own, first, second, roots, inverse, far, trailing)
    return updated, rows_shard.T, factor_shard.T


def solution(mesh):
    in_specs = (P("prow", None), P(), P("prow", "pcol"))
    out_specs = (P("prow", "pcol"), P("prow", "pcol"), P(None, "pcol"))
    return jax.shard_map(body, mesh=mesh, in_specs=in_specs, out_specs=out_specs, check_vma=False)
```
